32 devices in a mesh: freq: 4 (over x, core), rows: 8 (over z, y).
Axes of the slice: x: 2, y: 2, z: 4, core: 2. Of those that a mesh axis runs over, the one named last changes fastest.
Arguments:
- time_loads: float32 [256, 192, 2048], P('freq', None, 'rows'), may hold values from -6 to 6
- factor: float32 [16, 2, 2048, 2048], P('freq', None, 'rows'), may hold values from -0.09375 to 0.09375
- diag_inverse: float32 [16, 2, 2048, 256], P('freq', None, 'rows'), may hold values from -0.25 to 0.25
- pivot_order: int32 [8], replicated, may hold values from 0 to 7, each once
Outputs:
- solution: float32 [16, 2, 192, 2048], P('freq', None, None, 'rows')
The draws below stay inside these ranges and needn't reach their ends.
Inputs may be any that keep to these rules, and one draw needn't show every extreme that they name: `pivot_order`: a permutation of the 8 row blocks.
All inputs are finite; a program needn't handle non-finite values.
Results may differ from the reference program's by a relative error of at most 0.0001.
Values sent between devices are 32-bit elements; how exact they have to be, the bound alone decides.
A program may use at most 128 MiB of HBM per device.

```python
import jax
import jax.numpy as jnp
from jax import lax

BS = 256
FREQS = 16
STEPS = 256
CASES = 192
NB = 8
ROWS = 2048


def block_scale(stream_key, dims, shards, low, high):
    def one(position, shards_of):
        draws = jax.random.uniform(jax.random.fold_in(jax.random.fold_in(stream_key, 6), position), (shards_of,), jnp.float32, low / len(shards), high / len(shards))
        return jnp.repeat(jnp.exp(draws), dims[position] // shards_of).reshape((-1,) + (1,) * (len(dims) - position - 1))

    level = one(*shards[0])
    for cut in shards[1:]:
        level = level * one(*cut)
    return level


def gaussian(rng, extent, scale, reach, shards=(), held_as=jnp.bfloat16):
    gain = block_scale(rng, extent, shards, -0.22, 0.18) if shards else 1.0
    array = jax.random.normal(rng, extent, jnp.float32) * scale * gain
    return jnp.minimum(jnp.maximum(array, -reach), reach).astype(held_as)


def setup_inputs(seed: int = 0) -> dict:
    splits = jax.random.split(jax.random.key(seed), 5)
    return {
        "time_loads": gaussian(splits[0], (STEPS, CASES, ROWS), 1.0, 6.0, ((0, 4), (2, 8)), jnp.float32),
        "factor": gaussian(splits[1], (FREQS, 2, ROWS, ROWS), (2 * ROWS) ** -0.5, 0.09375, ((0, 4), (2, 8)), jnp.float32),
        "diag_inverse": gaussian(splits[2], (FREQS, 2, ROWS, BS), (2 * BS) ** -0.5, 0.25, ((0, 4), (2, 8)), jnp.float32),
        "pivot_order": jax.random.permutation(splits[3], NB).astype(jnp.int32),
    }


def tables(count, length):
    freq_range = jnp.arange(count, dtype=jnp.float32)
    step_range = jnp.arange(length, dtype=jnp.float32)
    angles = 2.0 * jnp.pi * ((freq_range[:, None] * step_range[None, :]) % length) / length
    damping = jnp.exp(step_range * (jnp.log(0.1) / length))
    return jnp.cos(angles) * damping[None, :], -jnp.sin(angles) * damping[None, :]


def product(matrix, vector):
    return jnp.einsum("fab,fcb->fca", matrix, vector, precision=lax.Precision.HIGHEST)


def complex_apply(matrix, vector):
    matrix_real, matrix_imag = matrix[:, 0], matrix[:, 1]
    vector_real, vector_imag = vector[:, 0], vector[:, 1]
    real_part = product(matrix_real, vector_real) - product(matrix_imag, vector_imag)
    imag_part = product(matrix_real, vector_imag) + product(matrix_imag, vector_real)
    return jnp.stack([real_part, imag_part], axis=1)


def reference(time_loads, factor, diag_inverse, pivot_order):
    cosine_table, sine_table = tables(FREQS, STEPS)
    spectra = jnp.stack([
        jnp.einsum("fn,ncr->fcr", cosine_table, time_loads, precision=lax.Precision.HIGHEST),
        jnp.einsum("fn,ncr->fcr", sine_table, time_loads, precision=lax.Precision.HIGHEST)], axis=1)
    residual = spectra
    solution = jnp.zeros_like(spectra)
    for turn in range(NB):
        first_row = (pivot_order[turn] * BS).astype(jnp.int32)
        current = lax.dynamic_slice_in_dim(residual, first_row, BS, 3)
        inverse_block = lax.dynamic_slice_in_dim(diag_inverse, first_row, BS, 2)
        solved = complex_apply(inverse_block, current)
        solution = lax.dynamic_update_slice_in_dim(solution, solved, first_row, 3)
        column = lax.dynamic_slice_in_dim(factor, first_row, BS, 3)
        residual = residual - complex_apply(column, solved)
    return solution
```

```python
import functools

import jax
import jax.numpy as jnp
from jax import lax
from jax.experimental import pallas as pl
from jax.experimental.pallas import tpu as pltpu
from jax.sharding import PartitionSpec as P

MESH = pl.DeviceIdType.MESH
LEAD = 2
LANES = 128


def tables(count, length):
    freq_range = jnp.arange(count, dtype=jnp.float32)
    step_range = jnp.arange(length, dtype=jnp.float32)
    angles = 2.0 * jnp.pi * (freq_range[:, None] * step_range[None, :] % length) / length
    damping = jnp.exp(step_range * (jnp.log(0.1) / length))
    return (jnp.cos(angles) * damping[None, :], -jnp.sin(angles) * damping[None, :])


def zigzag(major, minor, extent):
    return minor + lax.rem(major, 2) * (extent - 1 - 2 * minor)


def chain_position(kind, index, outer, inner):
    z, y = lax.div(index, inner), lax.rem(index, inner)
    if kind == 1:
        y = inner - 1 - y
    if kind == 3:
        z = outer - 1 - z
    if kind < 2:
        return z * inner + zigzag(z, y, inner)
    return y * outer + zigzag(y, z, outer)


def chain_index(kind, position, outer, inner):
    if kind < 2:
        z = lax.div(position, inner)
        y = zigzag(z, lax.rem(position, inner), inner)
    else:
        y = lax.div(position, outer)
        z = zigzag(y, lax.rem(position, outer), outer)
    if kind == 1:
        y = inner - 1 - y
    if kind == 3:
        z = outer - 1 - z
    return z * inner + y


def split(value):
    high = value.astype(jnp.bfloat16)
    return high, (value - high.astype(jnp.float32)).astype(jnp.bfloat16)


def triple(value, right_high, right_low):
    high, low = split(value)
    count = value.shape[0]
    both = jnp.dot(
        jnp.concatenate([high, low], axis=0), right_high, preferred_element_type=jnp.float32
    )
    rest = jnp.dot(high, right_low, preferred_element_type=jnp.float32)
    return both[:count] + both[count:] + rest


def whole(dims, pivot_ref, table_ref, loads_ref, factor_ref, inverse_ref, out_ref,
          loads, spectra, core_buf, chip_buf, taken, inverse, inverse_high, inverse_low,
          scaled_high, scaled_low, right_buf, left_buf,
          load_sem, factor_sem, inverse_sem, core_send, core_recv, chip_send, chip_recv,
          send_sem, recv_sem, pace_sem):
    freqs, blocks, units, cases, outer, inner, owners, steps = dims
    width = out_ref.shape[3]
    all_cases = units * cases
    chips = owners // 2
    rank = lax.axis_index("freq")
    chip, core = lax.div(rank, 2), lax.rem(rank, 2)
    partner = chip * 2 + 1 - core
    me = lax.axis_index("rows")
    slots = right_buf.shape[1]
    last = blocks - 1
    pieces = last * units
    group = owners * freqs * 2
    share = freqs * 2 * cases
    parts = load_sem.shape[0]
    halves = width // LANES
    part_rows = steps * halves // parts * all_cases

    def load_copy(part):
        half, rows = part % halves, pl.ds(part // halves * part_rows, part_rows)
        return pltpu.make_async_copy(
            loads_ref.at[rows, pl.ds(half * LANES, LANES)], loads.at[half, rows], load_sem.at[part]
        )

    def factor_copy(block):
        columns = pl.ds(block * width, width)
        return pltpu.make_async_copy(
            factor_ref.at[:, :, :, columns], taken.at[block], factor_sem.at[block]
        )

    inverse_copy = pltpu.make_async_copy(inverse_ref, inverse, inverse_sem)

    for part in range(parts):
        load_copy(part).start()
    inverse_copy.start()
    for block in range(blocks):
        factor_copy(block).start()

    barrier = pltpu.get_barrier_semaphore()
    for shift in range(1, blocks):
        pl.semaphore_signal(
            barrier, inc=1, device_id={"rows": lax.rem(me + shift, blocks)}, device_id_type=MESH
        )
    pl.semaphore_signal(barrier, inc=1, device_id={"freq": partner}, device_id_type=MESH)
    for shift in range(1, chips):
        pl.semaphore_signal(
            barrier, inc=1, device_id={"freq": lax.rem(chip + shift, chips) * 2 + core},
            device_id_type=MESH,
        )

    def share_rows(owner, u):
        return pl.ds(pl.multiple_of((u * owners + owner) * share, 8), share)

    def core_copy(to_chip, u):
        return pltpu.make_async_remote_copy(
            src_ref=spectra.at[:, share_rows(to_chip * 2 + 1 - core, u)],
            dst_ref=core_buf.at[to_chip, u],
            send_sem=core_send.at[to_chip, u],
            recv_sem=core_recv.at[to_chip, u],
            device_id={"freq": partner},
            device_id_type=MESH,
        )

    def chip_copy(shift, u):
        to_chip = lax.rem(chip + shift, chips)
        slot = chips - 1 - shift
        return pltpu.make_async_remote_copy(
            src_ref=core_buf.at[to_chip, u],
            dst_ref=chip_buf.at[slot, u],
            send_sem=chip_send.at[slot, u],
            recv_sem=chip_recv.at[slot, u],
            device_id={"freq": to_chip * 2 + core},
            device_id_type=MESH,
        )

    weights = jnp.concatenate(
        [split(table_ref[:group, :])[0], split(table_ref[group:, :])[1]], axis=0
    )

    def transform(u):
        for c in range(cases):
            some = pl.ds(u * cases + c, steps, stride=all_cases)
            high, low = split(
                jnp.concatenate([loads[half, some, :] for half in range(halves)], axis=1)
            )
            both = jnp.dot(
                weights, jnp.concatenate([high, low], axis=0),
                preferred_element_type=jnp.float32,
            )
            total = both[:group] + both[group:]
            for half in range(halves):
                spectra[half, pl.ds(u * group * cases + c, group, stride=cases), :] = (
                    total[:, half * LANES:(half + 1) * LANES]
                )
        for shift in range(1, chips):
            core_copy(lax.rem(chip + shift, chips), u).start()
        core_copy(chip, u).start()

    def pass_on(u):
        for shift in range(1, chips):
            to_chip = lax.rem(chip + shift, chips)
            core_copy(to_chip, u).wait_recv()
            core_buf[to_chip, u] = (
                core_buf[to_chip, u] + spectra[:, share_rows(to_chip * 2 + core, u), :]
            )
            chip_copy(shift, u).start()

    for part in range(parts):
        load_copy(part).wait()
    pl.semaphore_wait(barrier, last + chips)

    def prologue(u, carry):
        transform(u)

        @pl.when(u >= 1)
        def _():
            pass_on(u - 1)

        return carry

    lax.fori_loop(0, units, prologue, 0)
    pass_on(jnp.int32(units - 1))

    def rows_of(piece):
        return pl.ds(pl.multiple_of(lax.rem(piece, units) * cases, 8), cases)

    def start(u):
        core_copy(chip, u).wait_recv()
        for shift in range(1, chips):
            chip_copy(shift, u).wait_recv()
        rows = rows_of(u)
        for f in range(freqs):
            some = pl.ds(f * 2 * cases, 2 * cases)
            mine = pl.ds(pl.multiple_of((u * owners + rank) * share + f * 2 * cases, 8), 2 * cases)
            value = spectra[:, mine, :] + core_buf[chip, u, :, some, :]
            for shift in range(1, chips):
                value = value + chip_buf[chips - 1 - shift, u, :, some, :]
            value = jnp.concatenate([value[half] for half in range(halves)], axis=1)
            solved = triple(value, inverse_high[f], inverse_low[f])
            out_ref[f, 0, rows, :] = solved[:cases, :width] - solved[cases:, width:]
            out_ref[f, 1, rows, :] = solved[:cases, width:] + solved[cases:, :width]

    def scale(f, turn):
        block = pivot_ref[turn]
        slot = lax.rem(turn, 2)
        turned = jnp.concatenate([taken[block, f, 0].T, taken[block, f, 1].T], axis=0)
        total = triple(turned, inverse_high[f], inverse_low[f])
        from_real, from_imag = total[:width], total[width:]
        real = from_real[:, :width] - from_imag[:, width:]
        imag = from_real[:, width:] + from_imag[:, :width]
        scaled_high[slot, f], scaled_low[slot, f] = split(jnp.concatenate([real, imag], axis=1))

    inverse_copy.wait()
    for f in range(freqs):
        inverse_high[f], inverse_low[f] = split(
            jnp.concatenate([inverse[f, 0].T, inverse[f, 1].T], axis=1)
        )
    for block in range(blocks):
        factor_copy(block).wait()
    for f in range(freqs):
        scale(f, jnp.int32(0))

    my_turn = jnp.int32(0)
    for turn in range(blocks):
        my_turn = my_turn + jnp.where(pivot_ref[turn] == me, turn, 0)

    def copy(direction, f, piece, target):
        buf = (right_buf, left_buf)[direction]
        slot = lax.rem(piece, slots)
        return pltpu.make_async_remote_copy(
            src_ref=buf.at[f, slot],
            dst_ref=buf.at[f, slot],
            send_sem=send_sem.at[direction, f, lax.rem(piece, 2)],
            recv_sem=recv_sem.at[direction, f, slot],
            device_id={"rows": target},
            device_id_type=MESH,
        )

    chains = []
    for f in range(freqs):
        kind = f % 4
        position = chain_position(kind, me, outer, inner)
        right = chain_index(kind, lax.rem(position + 1, blocks), outer, inner)
        left = chain_index(kind, lax.rem(position + last, blocks), outer, inner)
        chains.append((kind, position, right, left))

    def flow(direction, f, piece, target, is_first, is_last):
        buf = (right_buf, left_buf)[direction]
        slot = lax.rem(piece, slots)

        @pl.when((piece >= 0) & (piece < pieces))
        def _():
            @pl.when(jnp.logical_not(is_first))
            def _():
                copy(direction, f, piece, target).wait_recv()
                mine = pivot_ref[lax.div(piece, units)] == me
                buf[f, slot] = jnp.where(mine, out_ref[f, :, rows_of(piece), :], buf[f, slot])

            @pl.when(is_first)
            def _():
                buf[f, slot] = out_ref[f, :, rows_of(piece), :]

            @pl.when(jnp.logical_not(is_last))
            def _():
                @pl.when(piece >= 2)
                def _():
                    copy(direction, f, piece - 2, target).wait_send()

                copy(direction, f, piece, target).start()

    def finish(f, kind, position, piece):
        @pl.when((piece >= 0) & (piece < pieces))
        def _():
            turn = lax.div(piece, units)
            slot = lax.rem(piece, slots)
            owner = chain_position(kind, pivot_ref[turn], outer, inner)
            solved = jnp.where(owner <= position, right_buf[f, slot], left_buf[f, slot])
            half = lax.rem(turn, 2)
            total = triple(
                solved.reshape(2 * cases, width), scaled_high[half, f], scaled_low[half, f]
            )
            from_real, from_imag = total[:cases], total[cases:]
            real = from_real[:, :width] - from_imag[:, width:]
            imag = from_real[:, width:] + from_imag[:, :width]
            rows = rows_of(piece)
            open_still = turn < my_turn
            real_now, imag_now = out_ref[f, 0, rows, :], out_ref[f, 1, rows, :]
            out_ref[f, 0, rows, :] = jnp.where(open_still, real_now - real, real_now)
            out_ref[f, 1, rows, :] = jnp.where(open_still, imag_now - imag, imag_now)

            @pl.when((lax.rem(piece, units) == f * (units // freqs)) & (turn + 1 < last))
            def _():
                scale(f, turn + 1)

    def tick(t, carry):
        pl.semaphore_signal(pace_sem, inc=1, device_id={"freq": partner}, device_id_type=MESH)

        @pl.when(t >= LEAD)
        def _():
            pl.semaphore_wait(pace_sem, 1)

        @pl.when(t < units)
        def _():
            start(t)

        for f, (kind, position, right, left) in enumerate(chains):
            at_start, at_end = position == 0, position == last
            flow(0, f, t - position, right, at_start, at_end)
            flow(1, f, t - (last - position), left, at_end, at_start)
            finish(f, kind, position, t - jnp.maximum(position, last - position))
        return carry

    lax.fori_loop(0, pieces + last, tick, 0)
    pl.semaphore_wait(pace_sem, LEAD)

    for f, (kind, position, right, left) in enumerate(chains):
        for piece in (pieces - 2, pieces - 1):
            @pl.when(position < last)
            def _():
                copy(0, f, jnp.int32(piece), right).wait_send()

            @pl.when(position > 0)
            def _():
                copy(1, f, jnp.int32(piece), left).wait_send()

    def sent(u, carry):
        for to_chip in range(chips):
            core_copy(to_chip, u).wait_send()
        for shift in range(1, chips):
            chip_copy(shift, u).wait_send()
        return carry

    lax.fori_loop(0, units, sent, 0)


def body(time_loads, factor, diag_inverse, pivot_order):
    freqs = factor.shape[0]
    steps, all_cases, width = time_loads.shape
    blocks = lax.axis_size("rows")
    owners = lax.axis_size("freq")
    cosine_table, sine_table = tables(freqs * owners, steps * owners)
    table = jnp.stack([cosine_table, sine_table], axis=1)
    table = lax.dynamic_slice_in_dim(table, lax.axis_index("freq") * steps, steps, 2)
    table = table.reshape(-1, steps)
    table = jnp.concatenate([
        jnp.concatenate([table, table], axis=1),
        jnp.concatenate([table, jnp.zeros_like(table)], axis=1),
    ], axis=0)

    cases = 8
    for wider in range(8, all_cases + 1, 8):
        if all_cases % wider == 0 and all_cases // wider >= blocks:
            cases = wider
    units = all_cases // cases
    inner = 1
    while 4 * inner * inner <= blocks:
        inner *= 2
    slots = 2 * blocks
    chips = owners // 2
    share = freqs * 2 * cases
    dims = (freqs, blocks, units, cases, blocks // inner, inner, owners, steps)
    vmem = pl.BlockSpec(memory_space=pltpu.VMEM)
    anywhere = pl.BlockSpec(memory_space=pl.ANY)
    halves = width // LANES
    parts = 4 * halves
    dma = pltpu.SemaphoreType.DMA
    others = max(chips - 1, 1)
    return pl.pallas_call(
        functools.partial(whole, dims),
        out_shape=jax.ShapeDtypeStruct((freqs, 2, all_cases, width), jnp.float32),
        in_specs=[
            pl.BlockSpec(memory_space=pltpu.SMEM), vmem, anywhere, anywhere, anywhere,
        ],
        out_specs=vmem,
        scratch_shapes=[
            pltpu.VMEM((halves, steps * all_cases, LANES), jnp.float32),
            pltpu.VMEM((halves, units * owners * share, LANES), jnp.float32),
            pltpu.VMEM((chips, units, halves, share, LANES), jnp.float32),
            pltpu.VMEM((others, units, halves, share, LANES), jnp.float32),
            pltpu.VMEM((blocks, freqs, 2, width, width), jnp.float32),
            pltpu.VMEM(diag_inverse.shape, jnp.float32),
            pltpu.VMEM((freqs, width, 2 * width), jnp.bfloat16),
            pltpu.VMEM((freqs, width, 2 * width), jnp.bfloat16),
            pltpu.VMEM((2, freqs, width, 2 * width), jnp.bfloat16),
            pltpu.VMEM((2, freqs, width, 2 * width), jnp.bfloat16),
            pltpu.VMEM((freqs, slots, 2, cases, width), jnp.float32),
            pltpu.VMEM((freqs, slots, 2, cases, width), jnp.float32),
            dma((parts,)), dma((blocks,)), dma,
            dma((chips, units)), dma((chips, units)), dma((others, units)), dma((others, units)),
            dma((2, freqs, 2)), dma((2, freqs, slots)),
            pltpu.SemaphoreType.REGULAR,
        ],
        compiler_params=pltpu.CompilerParams(
            collective_id=0, has_side_effects=True, vmem_limit_bytes=63 * 1024 * 1024,
        ),
    )(pivot_order, table, time_loads.reshape(steps * all_cases, width), factor, diag_inverse)


def solution(mesh):
    placed = (
        P("freq", None, "rows"),
        P("freq", None, "rows", None),
        P("freq", None, "rows", None),
        P(),
    )
    return jax.shard_map(
        body, mesh=mesh, in_specs=placed, out_specs=P("freq", None, None, "rows"), check_vma=False
    )
```

```python
import functools

import jax
import jax.numpy as jnp
from jax import lax
from jax.experimental import pallas as pl
from jax.experimental.pallas import tpu as pltpu
from jax.sharding import PartitionSpec as P

MESH = pl.DeviceIdType.MESH
LEAD = 2
STAGES = 3
LANES = 128


def tables(count, length):
    freq_range = jnp.arange(count, dtype=jnp.float32)
    step_range = jnp.arange(length, dtype=jnp.float32)
    angles = 2.0 * jnp.pi * (freq_range[:, None] * step_range[None, :] % length) / length
    damping = jnp.exp(step_range * (jnp.log(0.1) / length))
    return (jnp.cos(angles) * damping[None, :], -jnp.sin(angles) * damping[None, :])


def comb(kind, outer, inner):
    def along_outer(z, y):
        return kind >= 2 or y == (inner - 1 + kind) // 2

    def along_inner(z, y):
        return kind < 2 or z == (outer - 3 + kind) // 2

    nodes = [(z, y) for z in range(outer) for y in range(inner)]
    neighbours = [{} for _ in nodes]
    for z, y in nodes:
        for port, (dz, dy) in enumerate(((1, 0), (-1, 0), (0, 1), (0, -1))):
            allowed = along_outer(z, y) if dz else along_inner(z, y)
            if allowed and 0 <= z + dz < outer and 0 <= y + dy < inner:
                port = 2 if dy and inner == 2 else port
                neighbours[z * inner + y][port] = (z + dz) * inner + y + dy
    return neighbours


def departure(neighbours, node, to):
    others = [other for other in neighbours[node].values() if other != to]
    return max([departure(neighbours, other, node) + 1 for other in others], default=0)


def side(neighbours, node, to):
    found = {to}
    for other in neighbours[to].values():
        if other != node:
            found |= side(neighbours, to, other)
    return found


def layout(kinds, outer, inner):
    plans = []
    for kind in range(kinds):
        neighbours = comb(kind % 4, outer, inner)
        sends = [
            {port: departure(neighbours, node, to) for port, to in ports.items()}
            for node, ports in enumerate(neighbours)
        ]
        takes = [
            {port: departure(neighbours, to, node) + 1 for port, to in ports.items()}
            for node, ports in enumerate(neighbours)
        ]
        toward = [
            [
                max([port for port, to in ports.items() if owner in side(neighbours, node, to)],
                    default=-1)
                for owner in range(len(neighbours))
            ]
            for node, ports in enumerate(neighbours)
        ]
        plans.append((neighbours, sends, takes, toward))
    return plans


def split(value):
    high = value.astype(jnp.bfloat16)
    return high, (value - high.astype(jnp.float32)).astype(jnp.bfloat16)


def triple(value, right_high, right_low):
    high, low = split(value)
    count = value.shape[0]
    both = jnp.dot(
        jnp.concatenate([high, low], axis=0), right_high, preferred_element_type=jnp.float32
    )
    rest = jnp.dot(high, right_low, preferred_element_type=jnp.float32)
    return both[:count] + both[count:] + rest


def whole(dims, plans, pivot_ref, toward_ref, table_ref, loads_ref, factor_ref, inverse_ref, out_ref,
          loads, spectra, core_buf, chip_buf, taken, inverse, inverse_high, inverse_low,
          scaled_high, scaled_low, taken_in, sent_out,
          load_sem, factor_sem, inverse_sem, core_send, core_recv, chip_send, chip_recv,
          send_sem, recv_sem, pace_sem):
    freqs, blocks, units, cases, hop, owners, steps = dims
    width = out_ref.shape[3]
    all_cases = units * cases
    chips = owners // 2
    rank = lax.axis_index("freq")
    chip, core = lax.div(rank, 2), lax.rem(rank, 2)
    partner = chip * 2 + 1 - core
    me = lax.axis_index("rows")
    ports, _, slots = taken_in.shape[:3]
    stages = sent_out.shape[2]
    reach = max(max(takes[node].values()) for _, _, takes, _ in plans for node in range(blocks))
    last = blocks - 1
    pieces = last * units
    group = owners * freqs * 2
    share = freqs * 2 * cases
    parts = load_sem.shape[0]
    halves = width // LANES
    part_rows = steps * halves // parts * all_cases

    def load_copy(part):
        half, rows = part % halves, pl.ds(part // halves * part_rows, part_rows)
        return pltpu.make_async_copy(
            loads_ref.at[rows, pl.ds(half * LANES, LANES)], loads.at[half, rows], load_sem.at[part]
        )

    def factor_copy(block):
        columns = pl.ds(block * width, width)
        return pltpu.make_async_copy(
            factor_ref.at[:, :, :, columns], taken.at[block], factor_sem.at[block]
        )

    inverse_copy = pltpu.make_async_copy(inverse_ref, inverse, inverse_sem)

    for part in range(parts):
        load_copy(part).start()
    inverse_copy.start()
    for block in range(blocks):
        factor_copy(block).start()

    barrier = pltpu.get_barrier_semaphore()
    for shift in range(1, blocks):
        pl.semaphore_signal(
            barrier, inc=1, device_id={"rows": lax.rem(me + shift, blocks)}, device_id_type=MESH
        )
    pl.semaphore_signal(barrier, inc=1, device_id={"freq": partner}, device_id_type=MESH)
    for shift in range(1, chips):
        pl.semaphore_signal(
            barrier, inc=1, device_id={"freq": lax.rem(chip + shift, chips) * 2 + core},
            device_id_type=MESH,
        )

    def share_rows(owner, u):
        return pl.ds(pl.multiple_of((u * owners + owner) * share, 8), share)

    def core_copy(to_chip, u):
        return pltpu.make_async_remote_copy(
            src_ref=spectra.at[:, share_rows(to_chip * 2 + 1 - core, u)],
            dst_ref=core_buf.at[to_chip, u],
            send_sem=core_send.at[to_chip, u],
            recv_sem=core_recv.at[to_chip, u],
            device_id={"freq": partner},
            device_id_type=MESH,
        )

    def chip_copy(shift, u):
        to_chip = lax.rem(chip + shift, chips)
        slot = chips - 1 - shift
        return pltpu.make_async_remote_copy(
            src_ref=core_buf.at[to_chip, u],
            dst_ref=chip_buf.at[slot, u],
            send_sem=chip_send.at[slot, u],
            recv_sem=chip_recv.at[slot, u],
            device_id={"freq": to_chip * 2 + core},
            device_id_type=MESH,
        )

    weights = jnp.concatenate(
        [split(table_ref[:group, :])[0], split(table_ref[group:, :])[1]], axis=0
    )

    def transform(u):
        for c in range(cases):
            some = pl.ds(u * cases + c, steps, stride=all_cases)
            high, low = split(
                jnp.concatenate([loads[half, some, :] for half in range(halves)], axis=1)
            )
            both = jnp.dot(
                weights, jnp.concatenate([high, low], axis=0),
                preferred_element_type=jnp.float32,
            )
            total = both[:group] + both[group:]
            for half in range(halves):
                spectra[half, pl.ds(u * group * cases + c, group, stride=cases), :] = (
                    total[:, half * LANES:(half + 1) * LANES]
                )
        for shift in range(1, chips):
            core_copy(lax.rem(chip + shift, chips), u).start()
        core_copy(chip, u).start()

    def pass_on(u):
        for shift in range(1, chips):
            to_chip = lax.rem(chip + shift, chips)
            core_copy(to_chip, u).wait_recv()
            core_buf[to_chip, u] = (
                core_buf[to_chip, u] + spectra[:, share_rows(to_chip * 2 + core, u), :]
            )
            chip_copy(shift, u).start()

    for part in range(parts):
        load_copy(part).wait()
    pl.semaphore_wait(barrier, last + chips)

    def prologue(u, carry):
        transform(u)

        @pl.when(u >= 1)
        def _():
            pass_on(u - 1)

        return carry

    lax.fori_loop(0, units, prologue, 0)
    pass_on(jnp.int32(units - 1))

    def rows_of(piece):
        return pl.ds(pl.multiple_of(lax.rem(piece, units) * cases, 8), cases)

    def start(u):
        core_copy(chip, u).wait_recv()
        for shift in range(1, chips):
            chip_copy(shift, u).wait_recv()
        rows = rows_of(u)
        for f in range(freqs):
            some = pl.ds(f * 2 * cases, 2 * cases)
            mine = pl.ds(pl.multiple_of((u * owners + rank) * share + f * 2 * cases, 8), 2 * cases)
            value = spectra[:, mine, :] + core_buf[chip, u, :, some, :]
            for shift in range(1, chips):
                value = value + chip_buf[chips - 1 - shift, u, :, some, :]
            value = jnp.concatenate([value[half] for half in range(halves)], axis=1)
            solved = triple(value, inverse_high[f], inverse_low[f])
            out_ref[f, 0, rows, :] = solved[:cases, :width] - solved[cases:, width:]
            out_ref[f, 1, rows, :] = solved[:cases, width:] + solved[cases:, :width]

    def scale(f, turn):
        block = pivot_ref[turn]
        slot = lax.rem(turn, 2)
        turned = jnp.concatenate([taken[block, f, 0].T, taken[block, f, 1].T], axis=0)
        total = triple(turned, inverse_high[f], inverse_low[f])
        from_real, from_imag = total[:width], total[width:]
        real = from_real[:, :width] - from_imag[:, width:]
        imag = from_real[:, width:] + from_imag[:, :width]
        scaled_high[slot, f], scaled_low[slot, f] = split(jnp.concatenate([real, imag], axis=1))

    inverse_copy.wait()
    for f in range(freqs):
        inverse_high[f], inverse_low[f] = split(
            jnp.concatenate([inverse[f, 0].T, inverse[f, 1].T], axis=1)
        )
    for block in range(blocks):
        factor_copy(block).wait()
    for f in range(freqs):
        scale(f, jnp.int32(0))

    my_turn = jnp.int32(0)
    for turn in range(blocks):
        my_turn = my_turn + jnp.where(pivot_ref[turn] == me, turn, 0)

    def here(values):
        value = jnp.int32(0)
        for node, entry in enumerate(values):
            if entry != 0:
                value = value + jnp.where(me == node, entry, 0)
        return value

    def opposite(port):
        return port if ports == 3 and port == 2 else port ^ 1

    def copy(f, port, piece, target):
        slot, stage = lax.rem(piece, slots), lax.rem(piece, stages)
        return pltpu.make_async_remote_copy(
            src_ref=sent_out.at[port, f, stage],
            dst_ref=taken_in.at[opposite(port), f, slot],
            send_sem=send_sem.at[port, f, stage],
            recv_sem=recv_sem.at[opposite(port), f, slot],
            device_id={"rows": target},
            device_id_type=MESH,
        )

    def arrival(f, port, piece, target):
        slot, stage = lax.rem(piece, slots), lax.rem(piece, stages)
        return pltpu.make_async_remote_copy(
            src_ref=sent_out.at[port, f, stage],
            dst_ref=taken_in.at[port, f, slot],
            send_sem=send_sem.at[port, f, stage],
            recv_sem=recv_sem.at[port, f, slot],
            device_id={"rows": target},
            device_id_type=MESH,
        )

    trees = []
    for neighbours, sends, takes, _ in plans:
        edges = []
        for port in range(ports):
            if any(port in node for node in neighbours):
                edges.append((
                    port,
                    here([int(port in node) for node in neighbours]) == 1,
                    here([node.get(port, 0) for node in neighbours]),
                    hop * here([node.get(port, 0) for node in sends]),
                    hop * here([node.get(port, 0) for node in takes]),
                ))
        trees.append((edges, hop * here([max(node.values()) for node in takes])))

    def lead_of(f, piece):
        return toward_ref[(f * blocks + me) * blocks + pivot_ref[lax.div(piece, units)]]

    def receive(f, edge, t):
        port, present, target, _, lag = edge
        piece = t - lag

        @pl.when(present & (piece >= 0) & (piece < pieces))
        def _():
            arrival(f, port, piece, target).wait_recv()

    def send(f, edges, edge, t):
        port, present, target, lag, _ = edge
        piece = t - lag

        @pl.when(present & (piece >= 0) & (piece < pieces))
        def _():
            slot, stage = lax.rem(piece, slots), lax.rem(piece, stages)
            lead = lead_of(f, piece)
            value = out_ref[f, :, rows_of(piece), :]
            for other, _, _, _, _ in edges:
                if other != port:
                    value = jnp.where(lead == other, taken_in[other, f, slot], value)

            @pl.when(piece >= stages)
            def _():
                copy(f, port, piece - stages, target).wait_send()

            sent_out[port, f, stage] = value
            copy(f, port, piece, target).start()

    def finish(f, edges, piece):
        @pl.when((piece >= 0) & (piece < pieces))
        def _():
            turn = lax.div(piece, units)
            slot = lax.rem(piece, slots)
            lead = lead_of(f, piece)
            solved = taken_in[edges[0][0], f, slot]
            for other, _, _, _, _ in edges[1:]:
                solved = jnp.where(lead == other, taken_in[other, f, slot], solved)
            half = lax.rem(turn, 2)
            total = triple(
                solved.reshape(2 * cases, width), scaled_high[half, f], scaled_low[half, f]
            )
            from_real, from_imag = total[:cases], total[cases:]
            real = from_real[:, :width] - from_imag[:, width:]
            imag = from_real[:, width:] + from_imag[:, :width]
            rows = rows_of(piece)
            open_still = turn < my_turn
            real_now, imag_now = out_ref[f, 0, rows, :], out_ref[f, 1, rows, :]
            out_ref[f, 0, rows, :] = jnp.where(open_still, real_now - real, real_now)
            out_ref[f, 1, rows, :] = jnp.where(open_still, imag_now - imag, imag_now)

            @pl.when((lax.rem(piece, units) == f * (units // freqs)) & (turn + 1 < last))
            def _():
                scale(f, turn + 1)

    def tick(t, carry):
        pl.semaphore_signal(pace_sem, inc=1, device_id={"freq": partner}, device_id_type=MESH)

        @pl.when(t >= LEAD)
        def _():
            pl.semaphore_wait(pace_sem, 1)

        @pl.when(t < units)
        def _():
            start(t)

        for f, (edges, lag) in enumerate(trees):
            for edge in edges:
                receive(f, edge, t)
            for edge in edges:
                send(f, edges, edge, t)
            finish(f, edges, t - lag)
        return carry

    lax.fori_loop(0, pieces + hop * reach, tick, 0)
    pl.semaphore_wait(pace_sem, LEAD)

    for f, (edges, _) in enumerate(trees):
        for port, present, target, _, _ in edges:
            @pl.when(present)
            def _():
                for piece in range(pieces - stages, pieces):
                    copy(f, port, jnp.int32(piece), target).wait_send()

    def sent(u, carry):
        for to_chip in range(chips):
            core_copy(to_chip, u).wait_send()
        for shift in range(1, chips):
            chip_copy(shift, u).wait_send()
        return carry

    lax.fori_loop(0, units, sent, 0)


def body(time_loads, factor, diag_inverse, pivot_order):
    freqs = factor.shape[0]
    steps, all_cases, width = time_loads.shape
    blocks = lax.axis_size("rows")
    owners = lax.axis_size("freq")
    cosine_table, sine_table = tables(freqs * owners, steps * owners)
    table = jnp.stack([cosine_table, sine_table], axis=1)
    table = lax.dynamic_slice_in_dim(table, lax.axis_index("freq") * steps, steps, 2)
    table = table.reshape(-1, steps)
    table = jnp.concatenate([
        jnp.concatenate([table, table], axis=1),
        jnp.concatenate([table, jnp.zeros_like(table)], axis=1),
    ], axis=0)

    inner = 1
    while 4 * inner * inner <= blocks:
        inner *= 2
    plans = layout(freqs, blocks // inner, inner)
    reach = max(max(node.values()) for _, _, takes, _ in plans for node in takes)
    hop, cases = 1, 8
    for wider in range(8, all_cases + 1, 8):
        if all_cases % wider == 0 and all_cases // wider > 2 * reach:
            hop, cases = 2, wider
    units = all_cases // cases
    ports = 3 if inner == 2 else 4
    slots = hop * (reach + 1) + 2
    toward = jnp.array([plan[3] for plan in plans], jnp.int32).reshape(-1)
    chips = owners // 2
    share = freqs * 2 * cases
    dims = (freqs, blocks, units, cases, hop, owners, steps)
    smem = pl.BlockSpec(memory_space=pltpu.SMEM)
    vmem = pl.BlockSpec(memory_space=pltpu.VMEM)
    anywhere = pl.BlockSpec(memory_space=pl.ANY)
    halves = width // LANES
    parts = 4 * halves
    dma = pltpu.SemaphoreType.DMA
    others = max(chips - 1, 1)
    return pl.pallas_call(
        functools.partial(whole, dims, plans),
        out_shape=jax.ShapeDtypeStruct((freqs, 2, all_cases, width), jnp.float32),
        in_specs=[
            smem, smem, vmem, anywhere, anywhere, anywhere,
        ],
        out_specs=vmem,
        scratch_shapes=[
            pltpu.VMEM((halves, steps * all_cases, LANES), jnp.float32),
            pltpu.VMEM((halves, units * owners * share, LANES), jnp.float32),
            pltpu.VMEM((chips, units, halves, share, LANES), jnp.float32),
            pltpu.VMEM((others, units, halves, share, LANES), jnp.float32),
            pltpu.VMEM((blocks, freqs, 2, width, width), jnp.float32),
            pltpu.VMEM(diag_inverse.shape, jnp.float32),
            pltpu.VMEM((freqs, width, 2 * width), jnp.bfloat16),
            pltpu.VMEM((freqs, width, 2 * width), jnp.bfloat16),
            pltpu.VMEM((2, freqs, width, 2 * width), jnp.bfloat16),
            pltpu.VMEM((2, freqs, width, 2 * width), jnp.bfloat16),
            pltpu.VMEM((ports, freqs, slots, 2, cases, width), jnp.float32),
            pltpu.VMEM((ports, freqs, STAGES, 2, cases, width), jnp.float32),
            dma((parts,)), dma((blocks,)), dma,
            dma((chips, units)), dma((chips, units)), dma((others, units)), dma((others, units)),
            dma((ports, freqs, STAGES)), dma((ports, freqs, slots)),
            pltpu.SemaphoreType.REGULAR,
        ],
        compiler_params=pltpu.CompilerParams(
            collective_id=0, has_side_effects=True, vmem_limit_bytes=63 * 1024 * 1024,
        ),
    )(pivot_order, toward, table, time_loads.reshape(steps * all_cases, width), factor, diag_inverse)


def solution(mesh):
    placed = (
        P("freq", None, "rows"),
        P("freq", None, "rows", None),
        P("freq", None, "rows", None),
        P(),
    )
    return jax.shard_map(
        body, mesh=mesh, in_specs=placed, out_specs=P("freq", None, None, "rows"), check_vma=False
    )
```

```python
import functools

import jax
import jax.numpy as jnp
from jax import lax
from jax.experimental import pallas as pl
from jax.experimental.pallas import tpu as pltpu
from jax.sharding import PartitionSpec as P

MESH = pl.DeviceIdType.MESH
LEAD = 2
STAGES = 3
LANES = 128


def tables(count, length):
    freq_range = jnp.arange(count, dtype=jnp.float32)
    step_range = jnp.arange(length, dtype=jnp.float32)
    angles = 2.0 * jnp.pi * (freq_range[:, None] * step_range[None, :] % length) / length
    damping = jnp.exp(step_range * (jnp.log(0.1) / length))
    return (jnp.cos(angles) * damping[None, :], -jnp.sin(angles) * damping[None, :])


def comb(kind, outer, inner):
    def along_outer(z, y):
        return kind >= 2 or y == (inner - 1 + kind) // 2

    def along_inner(z, y):
        return kind < 2 or z == (outer - 3 + kind) // 2

    nodes = [(z, y) for z in range(outer) for y in range(inner)]
    neighbours = [{} for _ in nodes]
    for z, y in nodes:
        for port, (dz, dy) in enumerate(((1, 0), (-1, 0), (0, 1), (0, -1))):
            allowed = along_outer(z, y) if dz else along_inner(z, y)
            if allowed and 0 <= z + dz < outer and 0 <= y + dy < inner:
                port = 2 if dy and inner == 2 else port
                neighbours[z * inner + y][port] = (z + dz) * inner + y + dy
    return neighbours


def departure(neighbours, node, to):
    others = [other for other in neighbours[node].values() if other != to]
    return max([departure(neighbours, other, node) + 1 for other in others], default=0)


def side(neighbours, node, to):
    found = {to}
    for other in neighbours[to].values():
        if other != node:
            found |= side(neighbours, to, other)
    return found


def layout(kinds, outer, inner):
    plans = []
    for kind in range(kinds):
        neighbours = comb(kind % 4, outer, inner)
        sends = [
            {port: departure(neighbours, node, to) for port, to in ports.items()}
            for node, ports in enumerate(neighbours)
        ]
        takes = [
            {port: departure(neighbours, to, node) + 1 for port, to in ports.items()}
            for node, ports in enumerate(neighbours)
        ]
        toward = [
            [
                max([port for port, to in ports.items() if owner in side(neighbours, node, to)],
                    default=-1)
                for owner in range(len(neighbours))
            ]
            for node, ports in enumerate(neighbours)
        ]
        plans.append((neighbours, sends, takes, toward))
    return plans


def split(value):
    high = value.astype(jnp.bfloat16)
    return high, (value - high.astype(jnp.float32)).astype(jnp.bfloat16)


def triple(value, right_high, right_low):
    high, low = split(value)
    count = value.shape[0]
    both = jnp.dot(
        jnp.concatenate([high, low], axis=0), right_high, preferred_element_type=jnp.float32
    )
    rest = jnp.dot(high, right_low, preferred_element_type=jnp.float32)
    return both[:count] + both[count:] + rest


def whole(dims, plans, pivot_ref, toward_ref, table_ref, loads_ref, factor_ref, inverse_ref, out_ref,
          loads, spectra, core_buf, chip_buf, taken, inverse, inverse_high, inverse_low,
          scaled_high, scaled_low, taken_in, sent_out,
          load_sem, factor_sem, inverse_sem, core_send, core_recv, chip_send, chip_recv,
          send_sem, recv_sem, pace_sem):
    freqs, blocks, units, cases, hop, owners, steps = dims
    width = out_ref.shape[3]
    chips = owners // 2
    rank = lax.axis_index("freq")
    chip, core = lax.div(rank, 2), lax.rem(rank, 2)
    partner = chip * 2 + 1 - core
    me = lax.axis_index("rows")
    ports, _, slots = taken_in.shape[:3]
    stages = sent_out.shape[2]
    reach = max(max(takes[node].values()) for _, _, takes, _ in plans for node in range(blocks))
    first_finish = hop * min(
        max(takes[node].values()) for _, _, takes, _ in plans for node in range(blocks)
    )
    last = blocks - 1
    pieces = last * units
    group = owners * freqs * 2
    share = freqs * 2 * cases
    halves = width // LANES

    def here(values):
        value = jnp.int32(0)
        for node, entry in enumerate(values):
            if entry != 0:
                value = value + jnp.where(me == node, entry, 0)
        return value

    def rows_of(piece):
        return pl.ds(pl.multiple_of(lax.rem(jnp.int32(piece), units) * cases, 8), cases)

    def load_copy(half, u):
        return pltpu.make_async_copy(
            loads_ref.at[:, rows_of(u), pl.ds(half * LANES, LANES)], loads.at[half, u],
            load_sem.at[half, u],
        )

    def factor_copy(block):
        columns = pl.ds(block * width, width)
        return pltpu.make_async_copy(
            factor_ref.at[:, :, :, columns], taken.at[block], factor_sem.at[block]
        )

    inverse_copy = pltpu.make_async_copy(inverse_ref, inverse, inverse_sem)

    for u in range(units):
        for half in range(halves):
            load_copy(half, u).start()
    inverse_copy.start()

    barrier = pltpu.get_barrier_semaphore()
    friends = [sorted({to for plan in plans for to in plan[0][node].values()})
               for node in range(blocks)]
    for place in range(max(map(len, friends))):
        @pl.when(here([int(place < len(known)) for known in friends]) == 1)
        def _():
            friend = here([known[place] if place < len(known) else 0 for known in friends])
            pl.semaphore_signal(barrier, inc=1, device_id={"rows": friend}, device_id_type=MESH)
    pl.semaphore_signal(barrier, inc=1, device_id={"freq": partner}, device_id_type=MESH)
    for shift in range(1, chips):
        pl.semaphore_signal(
            barrier, inc=1, device_id={"freq": lax.rem(chip + shift, chips) * 2 + core},
            device_id_type=MESH,
        )

    def share_rows(owner, u):
        return pl.ds(pl.multiple_of((u * owners + owner) * share, 8), share)

    def core_copy(to_chip, u):
        return pltpu.make_async_remote_copy(
            src_ref=spectra.at[:, share_rows(to_chip * 2 + 1 - core, u)],
            dst_ref=core_buf.at[to_chip, u],
            send_sem=core_send.at[to_chip, u],
            recv_sem=core_recv.at[to_chip, u],
            device_id={"freq": partner},
            device_id_type=MESH,
        )

    def chip_copy(shift, u):
        to_chip = lax.rem(chip + shift, chips)
        slot = chips - 1 - shift
        return pltpu.make_async_remote_copy(
            src_ref=core_buf.at[to_chip, u],
            dst_ref=chip_buf.at[slot, u],
            send_sem=chip_send.at[slot, u],
            recv_sem=chip_recv.at[slot, u],
            device_id={"freq": to_chip * 2 + core},
            device_id_type=MESH,
        )

    weights = jnp.concatenate(
        [split(table_ref[:group, :])[0], split(table_ref[group:, :])[1]], axis=0
    )

    def transform(u):
        for half in range(halves):
            load_copy(half, u).wait()
        flat = [
            loads.at[half].reshape(units * steps * cases, LANES) for half in range(halves)
        ]
        for c in range(cases):
            some = pl.ds(u * steps * cases + c, steps, stride=cases)
            high, low = split(jnp.concatenate([part[some, :] for part in flat], axis=1))
            both = jnp.dot(
                weights, jnp.concatenate([high, low], axis=0),
                preferred_element_type=jnp.float32,
            )
            total = both[:group] + both[group:]
            for half in range(halves):
                spectra[half, pl.ds(u * group * cases + c, group, stride=cases), :] = (
                    total[:, half * LANES:(half + 1) * LANES]
                )

    def hand_over(u):
        for shift in range(1, chips):
            core_copy(lax.rem(chip + shift, chips), u).start()
        core_copy(chip, u).start()

    def pass_on(u):
        for shift in range(1, chips):
            to_chip = lax.rem(chip + shift, chips)
            core_copy(to_chip, u).wait_recv()
            core_buf[to_chip, u] = (
                core_buf[to_chip, u] + spectra[:, share_rows(to_chip * 2 + core, u), :]
            )
            chip_copy(shift, u).start()


    def prologue(u, carry):
        transform(u)

        @pl.when(u == 0)
        def _():
            pl.semaphore_wait(barrier, here([len(known) for known in friends]) + chips)

        hand_over(u)

        @pl.when(u >= 1)
        def _():
            pass_on(u - 1)

        @pl.when(u == units // 3)
        def _():
            for block in range(blocks):
                factor_copy(block).start()
            inverse_copy.wait()
            for f in range(freqs):
                inverse_high[f], inverse_low[f] = split(
                    jnp.concatenate([inverse[f, 0].T, inverse[f, 1].T], axis=1)
                )

        return carry

    lax.fori_loop(0, units, prologue, 0)
    pass_on(jnp.int32(units - 1))

    def start(u):
        core_copy(chip, u).wait_recv()
        for shift in range(1, chips):
            chip_copy(shift, u).wait_recv()
        rows = rows_of(u)
        for f in range(freqs):
            some = pl.ds(f * 2 * cases, 2 * cases)
            mine = pl.ds(pl.multiple_of((u * owners + rank) * share + f * 2 * cases, 8), 2 * cases)
            value = spectra[:, mine, :] + core_buf[chip, u, :, some, :]
            for shift in range(1, chips):
                value = value + chip_buf[chips - 1 - shift, u, :, some, :]
            value = jnp.concatenate([value[half] for half in range(halves)], axis=1)
            solved = triple(value, inverse_high[f], inverse_low[f])
            out_ref[f, 0, rows, :] = solved[:cases, :width] - solved[cases:, width:]
            out_ref[f, 1, rows, :] = solved[:cases, width:] + solved[cases:, :width]

    def scale(f, turn):
        block = pivot_ref[turn]
        slot = lax.rem(turn, 2)
        turned = jnp.concatenate([taken[block, f, 0].T, taken[block, f, 1].T], axis=0)
        total = triple(turned, inverse_high[f], inverse_low[f])
        from_real, from_imag = total[:width], total[width:]
        real = from_real[:, :width] - from_imag[:, width:]
        imag = from_real[:, width:] + from_imag[:, :width]
        scaled_high[slot, f], scaled_low[slot, f] = split(jnp.concatenate([real, imag], axis=1))

    for block in range(blocks):
        factor_copy(block).wait()

    my_turn = jnp.int32(0)
    for turn in range(blocks):
        my_turn = my_turn + jnp.where(pivot_ref[turn] == me, turn, 0)

    def opposite(port):
        return port if ports == 3 and port == 2 else port ^ 1

    def copy(f, port, piece, target):
        slot, stage = lax.rem(piece, slots), lax.rem(piece, stages)
        return pltpu.make_async_remote_copy(
            src_ref=sent_out.at[port, f, stage],
            dst_ref=taken_in.at[opposite(port), f, slot],
            send_sem=send_sem.at[port, f, stage],
            recv_sem=recv_sem.at[opposite(port), f, slot],
            device_id={"rows": target},
            device_id_type=MESH,
        )

    def arrival(f, port, piece, target):
        slot, stage = lax.rem(piece, slots), lax.rem(piece, stages)
        return pltpu.make_async_remote_copy(
            src_ref=sent_out.at[port, f, stage],
            dst_ref=taken_in.at[port, f, slot],
            send_sem=send_sem.at[port, f, stage],
            recv_sem=recv_sem.at[port, f, slot],
            device_id={"rows": target},
            device_id_type=MESH,
        )

    trees = []
    for neighbours, sends, takes, _ in plans:
        edges = []
        for port in range(ports):
            if any(port in node for node in neighbours):
                edges.append((
                    port,
                    here([int(port in node) for node in neighbours]) == 1,
                    here([node.get(port, 0) for node in neighbours]),
                    hop * here([node.get(port, 0) for node in sends]),
                    hop * here([node.get(port, 0) for node in takes]),
                ))
        trees.append((edges, hop * here([max(node.values()) for node in takes])))

    def lead_of(f, piece):
        return toward_ref[(f * blocks + me) * blocks + pivot_ref[lax.div(piece, units)]]

    def receive(f, edge, t):
        port, present, target, _, lag = edge
        piece = t - lag

        @pl.when(present & (piece >= 0) & (piece < pieces))
        def _():
            arrival(f, port, piece, target).wait_recv()

    def send(f, edges, edge, t):
        port, present, target, lag, _ = edge
        piece = t - lag

        @pl.when(present & (piece >= 0) & (piece < pieces))
        def _():
            slot, stage = lax.rem(piece, slots), lax.rem(piece, stages)
            lead = lead_of(f, piece)
            value = out_ref[f, :, rows_of(piece), :]
            for other, _, _, _, _ in edges:
                if other != port:
                    value = jnp.where(lead == other, taken_in[other, f, slot], value)

            @pl.when(piece >= stages)
            def _():
                copy(f, port, piece - stages, target).wait_send()

            sent_out[port, f, stage] = value
            copy(f, port, piece, target).start()

    def finish(f, edges, piece):
        @pl.when((piece >= 0) & (piece < pieces))
        def _():
            turn = lax.div(piece, units)
            slot = lax.rem(piece, slots)
            lead = lead_of(f, piece)
            solved = taken_in[edges[0][0], f, slot]
            for other, _, _, _, _ in edges[1:]:
                solved = jnp.where(lead == other, taken_in[other, f, slot], solved)
            half = lax.rem(turn, 2)
            total = triple(
                solved.reshape(2 * cases, width), scaled_high[half, f], scaled_low[half, f]
            )
            from_real, from_imag = total[:cases], total[cases:]
            real = from_real[:, :width] - from_imag[:, width:]
            imag = from_real[:, width:] + from_imag[:, :width]
            rows = rows_of(piece)
            open_still = turn < my_turn
            real_now, imag_now = out_ref[f, 0, rows, :], out_ref[f, 1, rows, :]
            out_ref[f, 0, rows, :] = jnp.where(open_still, real_now - real, real_now)
            out_ref[f, 1, rows, :] = jnp.where(open_still, imag_now - imag, imag_now)

    def prepare(f, piece):
        ahead = piece + first_finish - f
        turn = lax.div(ahead, units)

        @pl.when((ahead >= 0) & (lax.rem(ahead, units) == 0) & (turn < last))
        def _():
            scale(f, turn)

    def tick(t, carry):
        pl.semaphore_signal(pace_sem, inc=1, device_id={"freq": partner}, device_id_type=MESH)

        @pl.when(t >= LEAD)
        def _():
            pl.semaphore_wait(pace_sem, 1)

        @pl.when(t < units)
        def _():
            start(t)

        for f, (edges, lag) in enumerate(trees):
            for edge in edges:
                receive(f, edge, t)
            for edge in edges:
                send(f, edges, edge, t)
            prepare(f, t - lag)
            finish(f, edges, t - lag)
        return carry

    lax.fori_loop(0, pieces + hop * reach, tick, 0)
    pl.semaphore_wait(pace_sem, LEAD)

    for f, (edges, _) in enumerate(trees):
        for port, present, target, _, _ in edges:
            @pl.when(present)
            def _():
                for piece in range(pieces - stages, pieces):
                    copy(f, port, jnp.int32(piece), target).wait_send()

    def sent(u, carry):
        for to_chip in range(chips):
            core_copy(to_chip, u).wait_send()
        for shift in range(1, chips):
            chip_copy(shift, u).wait_send()
        return carry

    lax.fori_loop(0, units, sent, 0)


def body(time_loads, factor, diag_inverse, pivot_order):
    freqs = factor.shape[0]
    steps, all_cases, width = time_loads.shape
    blocks = lax.axis_size("rows")
    owners = lax.axis_size("freq")
    cosine_table, sine_table = tables(freqs * owners, steps * owners)
    table = jnp.stack([cosine_table, sine_table], axis=1)
    table = lax.dynamic_slice_in_dim(table, lax.axis_index("freq") * steps, steps, 2)
    table = table.reshape(-1, steps)
    table = jnp.concatenate([
        jnp.concatenate([table, table], axis=1),
        jnp.concatenate([table, jnp.zeros_like(table)], axis=1),
    ], axis=0)

    inner = 1
    while 4 * inner * inner <= blocks:
        inner *= 2
    plans = layout(freqs, blocks // inner, inner)
    reach = max(max(node.values()) for _, _, takes, _ in plans for node in takes)
    hop, cases = 1, 8
    for wider in range(8, all_cases + 1, 8):
        if all_cases % wider == 0 and all_cases // wider > 2 * reach:
            hop, cases = 2, wider
    units = all_cases // cases
    ports = 3 if inner == 2 else 4
    slots = hop * (reach + 1) + 2
    toward = jnp.array([plan[3] for plan in plans], jnp.int32).reshape(-1)
    chips = owners // 2
    share = freqs * 2 * cases
    dims = (freqs, blocks, units, cases, hop, owners, steps)
    smem = pl.BlockSpec(memory_space=pltpu.SMEM)
    vmem = pl.BlockSpec(memory_space=pltpu.VMEM)
    anywhere = pl.BlockSpec(memory_space=pl.ANY)
    halves = width // LANES
    dma = pltpu.SemaphoreType.DMA
    others = max(chips - 1, 1)
    return pl.pallas_call(
        functools.partial(whole, dims, plans),
        out_shape=jax.ShapeDtypeStruct((freqs, 2, all_cases, width), jnp.float32),
        in_specs=[
            smem, smem, vmem, anywhere, anywhere, anywhere,
        ],
        out_specs=vmem,
        scratch_shapes=[
            pltpu.VMEM((halves, units, steps, cases, LANES), jnp.float32),
            pltpu.VMEM((halves, units * owners * share, LANES), jnp.float32),
            pltpu.VMEM((chips, units, halves, share, LANES), jnp.float32),
            pltpu.VMEM((others, units, halves, share, LANES), jnp.float32),
            pltpu.VMEM((blocks, freqs, 2, width, width), jnp.float32),
            pltpu.VMEM(diag_inverse.shape, jnp.float32),
            pltpu.VMEM((freqs, width, 2 * width), jnp.bfloat16),
            pltpu.VMEM((freqs, width, 2 * width), jnp.bfloat16),
            pltpu.VMEM((2, freqs, width, 2 * width), jnp.bfloat16),
            pltpu.VMEM((2, freqs, width, 2 * width), jnp.bfloat16),
            pltpu.VMEM((ports, freqs, slots, 2, cases, width), jnp.float32),
            pltpu.VMEM((ports, freqs, STAGES, 2, cases, width), jnp.float32),
            dma((halves, units)), dma((blocks,)), dma,
            dma((chips, units)), dma((chips, units)), dma((others, units)), dma((others, units)),
            dma((ports, freqs, STAGES)), dma((ports, freqs, slots)),
            pltpu.SemaphoreType.REGULAR,
        ],
        compiler_params=pltpu.CompilerParams(
            collective_id=0, has_side_effects=True, vmem_limit_bytes=63 * 1024 * 1024,
        ),
    )(pivot_order, toward, table, time_loads, factor, diag_inverse)


def solution(mesh):
    placed = (
        P("freq", None, "rows"),
        P("freq", None, "rows", None),
        P("freq", None, "rows", None),
        P(),
    )
    return jax.shard_map(
        body, mesh=mesh, in_specs=placed, out_specs=P("freq", None, None, "rows"), check_vma=False
    )
```
